32 devices in a mesh: seq: 8 (over y, x, core), exp: 4 (over z).
Axes of the slice: x: 2, y: 2, z: 4, core: 2. Of those that a mesh axis runs over, the one named last changes fastest.
Arguments:
- queries: bfloat16 [4096, 2048], P('seq', 'exp'), may hold values from -6 to 6
- keys: bfloat16 [4096, 2048], P('seq', 'exp'), may hold values from -6 to 6
- values: bfloat16 [4096, 2048], P('seq', 'exp'), may hold values from -6 to 6
- head_gain: float32 [2048], P('exp'), may hold values from 0.5 to 1.5
- chosen: int32 [64, 3], replicated, may hold values from -1 to 55, as said below
- moe_input: bfloat16 [64, 7168], P('exp', 'seq'), may hold values from -6 to 6
- expert_ids: int32 [64, 2], P('exp'), may hold values from 0 to 3, all different within a row; in each aligned block of 16 rows (0 to 15, 16 to 31, ...) at most 12 rows name the same one
- route_weight: float32 [64, 2], P('exp'), may hold values from 0.05 to 0.5
- w_gate: bfloat16 [4, 7168, 2048], P('exp', 'seq'), may hold values from -0.09375 to 0.09375
- w_up: bfloat16 [4, 7168, 2048], P('exp', 'seq'), may hold values from -0.09375 to 0.09375
- w_down: bfloat16 [4, 2048, 7168], P('exp', None, 'seq'), may hold values from -0.125 to 0.125
Outputs:
- attention_out: bfloat16 [4096, 2048], P('seq', 'exp')
- moe_out: bfloat16 [64, 7168], P('exp', 'seq')
The draws below stay inside these ranges and needn't reach their ends.
Inputs may be any that keep to these rules, and one draw needn't show every extreme that they name: `chosen`: each entry names a group of an earlier segment than the query block's own, or is -1. The groups in one row lie in different segments; -1 stands exactly where the block's segment has fewer than 3 earlier segments, and then all of them are named. Query blocks of one segment that name groups of the same earlier segment name the same group of it. `expert_ids`: among the 16 rows of one index of exp, no expert is named by more than 12 rows.
All inputs are finite; a program needn't handle non-finite values.
Results may differ from the reference program's by a relative error of at most 0.0057.
Values may be sent and summed in bfloat16 or wider, within the bound.
A program may use at most 64 MiB of HBM per device.

```python
import math
import jax
import jax.numpy as jnp
import numpy as np
from jax import lax

D = 7168
FF = 2048
QK = 128
VD = 128
GROUP = 64
TOPK = 3
L_DEV = 512
TOK_E = 16
SEQ = 4096
HEADS = 16
EXPERTS = 4
TOP = 2
CAP = 12
TOKENS_M = 64


def draw_queries(key, part):
    drawn = jnp.clip(jax.random.normal(jax.random.fold_in(key, 11), (SEQ, HEADS * QK), jnp.float32), -6.0, 6.0)
    return drawn.astype(jnp.bfloat16)


def draw_keys(key, part):
    drawn = jnp.clip(jax.random.normal(jax.random.fold_in(key, 12), (SEQ, HEADS * QK), jnp.float32), -6.0, 6.0)
    return drawn.astype(jnp.bfloat16)


def draw_chosen(key, part):
    block_count = L_DEV // GROUP
    seg_count = SEQ // L_DEV
    all_blocks = SEQ // GROUP
    picked_group = jax.random.randint(jax.random.fold_in(key, 21), (seg_count, seg_count), 0, block_count)
    owner_rows = jnp.arange(seg_count, dtype=jnp.int32)[:, None]
    source_cols = jnp.arange(seg_count, dtype=jnp.int32)[None, :]
    final_pair = (owner_rows == seg_count - 1) & (source_cols == seg_count - 2)
    picked_group = jnp.where(final_pair, block_count - 1, picked_group)
    noise = jax.random.randint(jax.random.fold_in(key, 22), (all_blocks, seg_count), 0, 1 << 20)
    owner = jnp.arange(all_blocks, dtype=jnp.int32) // block_count
    sources = jnp.arange(seg_count, dtype=jnp.int32)
    boosted = (owner[:, None] == seg_count - 1) & (sources[None, :] == seg_count - 2)
    noise = jnp.where(boosted, 1 << 20, noise)
    earlier = sources[None, :] < owner[:, None]
    ranking = jnp.where(earlier, noise * seg_count + sources[None, :], sources[None, :] - seg_count)
    unused, leaders = lax.top_k(ranking, TOPK)
    valid = leaders < owner[:, None]
    group_index = leaders * block_count + picked_group[owner[:, None], leaders]
    return jnp.where(valid, group_index, -1).astype(jnp.int32)


def strengthened(result, key, source, target, blocks, factor):
    owner, partner = [(jnp.arange(result.shape[dim]) // (result.shape[dim] // blocks)).reshape([-1 if axis == dim else 1 for axis in range(result.ndim)]) for dim in (source, target)]
    chosen = jax.random.permutation(key, blocks)[partner]
    strong = (owner == chosen) | (owner == (partner + blocks // 2) % blocks)
    return jnp.where(strong, factor * result, result)


def block_scale(rng, shape, split, low, largest):
    level, own = 1.0, jax.random.fold_in(rng, 6)
    for position, blocks in split:
        heights = jnp.exp(jax.random.uniform(jax.random.fold_in(own, position), (blocks,), jnp.float32, low / len(split), largest / len(split)))
        level = level * jnp.repeat(heights, shape[position] // blocks).reshape([-1 if axis == position else 1 for axis in range(len(shape))])
    return level


def routed_block(stream_key, own, number, rows, number_of, top, reach, lean):
    order = jax.random.permutation(stream_key, number_of)
    crowded, usual = shares(number_of, rows * top, reach, lean, True), shares(number_of, rows * top, reach, lean, False)
    places = jnp.arange(number_of)

    def named(tallies, rotation):
        used = int((tallies > 0).sum())
        fixed = max(1, used // 4)
        passed = fixed + (places - fixed + rotation * (used - fixed)) % max(1, number_of - fixed)
        return jnp.zeros((number_of,), jnp.int32).at[order[jnp.where(places < fixed, places, passed)]].set(jnp.asarray(tallies, jnp.int32))

    tallies = jnp.where(number % 4 == 0, named(crowded, number // 4), named(usual, number - number // 4 - 1))
    mixed = jax.random.permutation(jax.random.fold_in(own, 3), number_of)
    giver, receiver = mixed[0:number_of // 2 * 2:2], mixed[1:number_of // 2 * 2:2]
    margin = jnp.minimum(tallies[giver] - 1, reach - tallies[receiver]) // 2
    margin = jnp.where((giver == order[0]) | (receiver == order[0]) | (tallies[receiver] == 0), 0, jnp.maximum(margin, 0))
    passed = jax.random.randint(jax.random.fold_in(own, 4), (number_of // 2,), 0, 1 << 20) % (margin + 1)
    tallies = tallies.at[giver].add(-passed).at[receiver].add(passed)
    items = jnp.searchsorted(jnp.cumsum(tallies), jnp.arange(rows * top), side="right").astype(jnp.int32)
    listing = items.reshape(top, rows).T
    listing = listing[jax.random.permutation(jax.random.fold_in(own, 1), rows)]
    rotation = jax.random.randint(jax.random.fold_in(own, 2), (rows, 1), 0, top)
    return jnp.take_along_axis(listing, (jnp.arange(top)[None, :] + rotation) % top, axis=1)


def shares(count, total, most, skew, full):
    weights = [(1 << 20) // math.isqrt(standing ** skew) + 1 for standing in range(1, count + 1)]
    largest = most if full else min(most, max(-(-total // count), total * weights[0] // sum(weights)))
    least = 1 if total - largest >= count - 1 else 0
    given, surplus = [largest] + [least] * (count - 1), total - largest - least * (count - 1)
    while surplus > 0:
        free = [i for i in range(1, count) if given[i] < largest] or [i for i in range(1, count) if given[i] < most]
        pool, left = sum([weights[i] for i in free]), surplus
        for i in free:
            more = min(most - given[i], max(1, left * weights[i] // pool), surplus)
            given[i] = given[i] + more
            surplus = surplus - more
    return np.array(given)


def bell_draw(key, extent, width, bound, cuts=(), held_as=jnp.bfloat16):
    result = width * jax.random.normal(key, extent, jnp.float32)
    if cuts:
        result = result * block_scale(key, extent, cuts, -0.22, 0.18)
    return jnp.clip(result, -bound, bound).astype(held_as)


def noise_with(stream_key, shape, spread, limit, shards, heavy, kind=jnp.bfloat16):
    result = spread * jax.random.normal(stream_key, shape, jnp.float32)
    if shards:
        result = result * block_scale(stream_key, shape, shards, -0.22, 0.18)
    return jnp.clip(strengthened(result, jax.random.fold_in(stream_key, 3), *heavy), -limit, limit).astype(kind)


def setup_inputs(seed: int = 0) -> dict:
    seeds = jax.random.split(jax.random.key(seed), 12)
    queries = draw_queries(jax.random.fold_in(seeds[11], 71), 0)
    keys = draw_keys(jax.random.fold_in(seeds[11], 71), 0)
    values = bell_draw(seeds[2], (SEQ, HEADS * VD), 1.0, 6.0, ((0, 8), (1, 4)))
    head_gain = jnp.clip(1.0 + 0.1 * jax.random.normal(seeds[3], (HEADS * VD,), jnp.float32), 0.5, 1.5)
    chosen = draw_chosen(jax.random.fold_in(seeds[11], 71), 0)
    moe_input = bell_draw(seeds[5], (TOKENS_M, D), 1.0, 6.0, ((0, 4), (1, 8)))
    expert_ids_keys = jax.random.split(jax.random.fold_in(seeds[6], 1), TOKENS_M // TOK_E)
    expert_ids_turns = jax.random.permutation(jax.random.fold_in(seeds[6], 3), TOKENS_M // TOK_E)
    expert_ids = jax.vmap(lambda own, number: routed_block(jax.random.fold_in(seeds[6], 2), own, number, TOK_E, EXPERTS, TOP, CAP, 2))(expert_ids_keys, expert_ids_turns).reshape((TOKENS_M, TOP))
    route_weight = jnp.clip(jnp.exp(math.log(0.5) - 2.3025851 * jax.random.uniform(seeds[7], (TOKENS_M, TOP), jnp.float32) ** block_scale(seeds[7], (TOKENS_M, TOP), ((0, 4),), -0.2, 0.2)), 0.05, 0.5)
    w_gate = noise_with(seeds[8], (EXPERTS, D, FF), D ** -0.5, 0.09375, ((0, 4), (1, 8)), (1, 2, 8, 2.0))
    w_up = noise_with(seeds[9], (EXPERTS, D, FF), D ** -0.5, 0.09375, ((0, 4), (1, 8)), (1, 2, 8, 2.0))
    w_down = bell_draw(seeds[10], (EXPERTS, FF, D), FF ** -0.5, 0.125, ((0, 4), (2, 8)))
    return dict(queries=queries, keys=keys, values=values, head_gain=head_gain, chosen=chosen, moe_input=moe_input, expert_ids=expert_ids, route_weight=route_weight, w_gate=w_gate, w_up=w_up, w_down=w_down)


EPSILON = 1e-06
NEGATIVE = -1e+30

def pool_groups(source):
    total = lax.optimization_barrier(jnp.sum(source.reshape(-1, GROUP, source.shape[1]).astype(jnp.float32), axis=1))
    return (total * GROUP ** (-0.5)).astype(jnp.bfloat16)

def heads_first(source, depth):
    return source.reshape(source.shape[0], -1, depth).transpose(1, 0, 2)

def head_attention(query_block_tiles, nearby_keys, nearby_values, compressed_keys, compressed_values, pool_mask, selected_keys, selected_values, picked_mask):
    block_count, block_width, depth = query_block_tiles.shape
    logit_scale = depth ** (-0.5)
    highest_accuracy = lax.Precision.HIGHEST
    query_wide_float = query_block_tiles.astype(jnp.float32)
    nearby_scores = jnp.einsum('rgo,uo->rgu', query_wide_float, nearby_keys.astype(jnp.float32), precision=highest_accuracy) * logit_scale
    query_pos = jnp.arange(block_count * block_width, dtype=jnp.int32).reshape(block_count, block_width)
    causal = query_pos[:, :, None] >= jnp.arange(nearby_keys.shape[0], dtype=jnp.int32)[None, None, :]
    nearby_scores = jnp.where(causal, nearby_scores, NEGATIVE)
    compressed_scores = jnp.einsum('nth,zh->ntz', query_wide_float, compressed_keys.astype(jnp.float32), precision=highest_accuracy) * logit_scale
    compressed_scores = jnp.where(pool_mask[None, None, :], compressed_scores, NEGATIVE)
    selected_scores = jnp.einsum('jae,jve->jav', query_wide_float, selected_keys.astype(jnp.float32), precision=highest_accuracy) * logit_scale
    selected_scores = jnp.where(picked_mask[:, None, :], selected_scores, NEGATIVE)
    highest = jnp.maximum(jnp.maximum(lax.optimization_barrier(jnp.max(nearby_scores, axis=-1)), lax.optimization_barrier(jnp.max(compressed_scores, axis=-1))), lax.optimization_barrier(jnp.max(selected_scores, axis=-1)))[:, :, None]
    nearby_probabilities = jnp.exp(nearby_scores - highest)
    compressed_probabilities = jnp.exp(compressed_scores - highest)
    selected_probabilities = jnp.exp(selected_scores - highest)
    denominator = lax.optimization_barrier(jnp.sum(nearby_probabilities, axis=-1)) + lax.optimization_barrier(jnp.sum(compressed_probabilities, axis=-1)) + lax.optimization_barrier(jnp.sum(selected_probabilities, axis=-1))
    blended_output = jnp.einsum('epc,cf->epf', nearby_probabilities.astype(jnp.bfloat16).astype(jnp.float32), nearby_values.astype(jnp.float32), precision=highest_accuracy)
    blended_output = blended_output + jnp.einsum('trx,xv->trv', compressed_probabilities.astype(jnp.bfloat16).astype(jnp.float32), compressed_values.astype(jnp.float32), precision=highest_accuracy)
    blended_output = blended_output + jnp.einsum('gvc,gcr->gvr', selected_probabilities.astype(jnp.bfloat16).astype(jnp.float32), selected_values.astype(jnp.float32), precision=highest_accuracy)
    return blended_output / denominator[:, :, None]

def head_norm(blended_output, gain):
    mean_square = lax.optimization_barrier(jnp.mean(blended_output * blended_output, axis=-1, keepdims=True))
    return (blended_output * lax.rsqrt(mean_square + EPSILON) * gain).astype(jnp.bfloat16)

def reference(queries, keys, values, head_gain, chosen, moe_input, expert_ids, route_weight, w_gate, w_up, w_down):
    seg_count = SEQ // L_DEV
    block_count = L_DEV // GROUP
    group_count = SEQ // GROUP
    compressed_keys = heads_first(pool_groups(keys), QK)
    compressed_values = heads_first(pool_groups(values), VD)
    gains = head_gain.reshape(-1, VD)
    within = jnp.arange(GROUP, dtype=jnp.int32)
    attend = jax.vmap(head_attention, in_axes=(0, 0, 0, 0, 0, None, 0, 0, None))

    def one_segment(segment):
        row_start = (segment * L_DEV).astype(jnp.int32)
        query_part = heads_first(lax.dynamic_slice_in_dim(queries, row_start, L_DEV, 0), QK)
        query_part = query_part.reshape(query_part.shape[0], block_count, GROUP, QK)
        nearby_keys = heads_first(lax.dynamic_slice_in_dim(keys, row_start, L_DEV, 0), QK)
        nearby_values = heads_first(lax.dynamic_slice_in_dim(values, row_start, L_DEV, 0), VD)
        chosen_rows = lax.dynamic_slice_in_dim(chosen, (segment * block_count).astype(jnp.int32), block_count, 0)
        token_index = (jnp.maximum(chosen_rows, 0)[:, :, None] * GROUP + within[None, None, :]).reshape(-1).astype(jnp.int32)
        selected_keys = heads_first(keys[token_index], QK).reshape(-1, block_count, TOPK * GROUP, QK)
        selected_values = heads_first(values[token_index], VD).reshape(-1, block_count, TOPK * GROUP, VD)
        picked_mask = jnp.repeat(chosen_rows >= 0, GROUP, axis=1)
        pool_mask = jnp.arange(group_count, dtype=jnp.int32) < segment * block_count
        blended_output = attend(query_part, nearby_keys, nearby_values, compressed_keys, compressed_values, pool_mask, selected_keys, selected_values, picked_mask)
        normed = head_norm(blended_output, gains[:, None, None, :])
        return normed.transpose(1, 2, 0, 3).reshape(L_DEV, -1)
    attention_out = lax.map(one_segment, jnp.arange(seg_count, dtype=jnp.int32)).reshape(SEQ, -1)
    expert_count = w_gate.shape[0]

    def one_expert(expert):
        gate = jnp.dot(moe_input, w_gate[expert], preferred_element_type=jnp.float32)
        upward = jnp.dot(moe_input, w_up[expert], preferred_element_type=jnp.float32)
        hidden = (jax.nn.silu(gate) * upward).astype(jnp.bfloat16)
        return jnp.dot(hidden, w_down[expert], preferred_element_type=jnp.float32).astype(jnp.bfloat16)
    expert_outs = lax.map(one_expert, jnp.arange(expert_count, dtype=jnp.int32))
    matches = (expert_ids[:, :, None] == jnp.arange(expert_count, dtype=jnp.int32)[None, None, :]).astype(jnp.float32)
    coefficient = lax.optimization_barrier(jnp.sum(route_weight[:, :, None] * matches, axis=1))
    moe_out = jnp.einsum('te,etd->td', coefficient, expert_outs.astype(jnp.float32), precision=lax.Precision.HIGHEST).astype(jnp.bfloat16)
    return (attention_out, moe_out)
```

```python
import functools

import jax
import jax.numpy as jnp
from jax import lax
from jax.experimental import pallas as pl
from jax.experimental.pallas import tpu as pltpu
from jax.sharding import PartitionSpec as P

HEAD = 128
GROUP = 64
TOPK = 3
TILE = 128
EPSILON = 1e-06
NEGATIVE = -1e30
MESH = pl.DeviceIdType.MESH
F32 = jnp.float32
BF16 = jnp.bfloat16


def across(a, b):
    return lax.dot_general(a, b, (((1,), (1,)), ((), ())), preferred_element_type=F32)


def kernel(
    S, E,
    q_ref, k_ref, v_ref, gain_ref, chosen_ref, x_ref, ids_ref, rw_ref, wg_hbm, wu_hbm, wd_hbm,
    attn_ref, moe_ref,
    wg, wu, wd, kv_send, kv_all, pool_send, pool_all, pool_k, pool_v,
    acc, top, den, x_all, part, rs_all, hid_send, hid_all, ret_send, ret_all,
    w_sem, kv_ss, kv_rs, pool_ss, pool_rs, x_ss, x_rs, rs_ss, rs_rs, hid_ss, hid_rs, ret_ss, ret_rs,
):
    me = lax.axis_index("seq")
    ex = lax.axis_index("exp")
    L, C = q_ref.shape
    heads = C // HEAD
    nb = L // GROUP
    T, Dl = x_ref.shape
    FF = wg.shape[1]
    rows = E * T
    own = rows // S
    scale = HEAD ** (-0.5)

    weight_copies = [
        pltpu.make_async_copy(src, dst, w_sem.at[i])
        for i, (src, dst) in enumerate(((wg_hbm, wg), (wu_hbm, wu), (wd_hbm, wd)))
    ]
    for copy in weight_copies:
        copy.start()

    def seq_copy(src, dst, ss, rs, peer):
        return pltpu.make_async_remote_copy(
            src_ref=src, dst_ref=dst, send_sem=ss, recv_sem=rs,
            device_id={"seq": peer}, device_id_type=MESH,
        )

    def exp_copy(src, dst, ss, rs, peer):
        return pltpu.make_async_remote_copy(
            src_ref=src, dst_ref=dst, send_sem=ss, recv_sem=rs,
            device_id={"exp": peer}, device_id_type=MESH,
        )

    def loop(low, high, body):
        def step(i, c):
            body(i)
            return c
        lax.fori_loop(low, high, step, 0)

    barrier = pltpu.get_barrier_semaphore()
    loop(1, E, lambda d: pl.semaphore_signal(
        barrier, inc=1, device_id={"exp": lax.rem(ex + d, E)}, device_id_type=MESH))
    loop(1, S, lambda d: pl.semaphore_signal(
        barrier, inc=1, device_id={"seq": lax.rem(me + d, S)}, device_id_type=MESH))

    total_k = jnp.sum(k_ref[...].astype(F32), axis=1)
    total_v = jnp.sum(v_ref[...].astype(F32), axis=1)
    pool_send[...] = (jnp.concatenate([total_k, total_v], axis=0) * GROUP ** (-0.5)).astype(BF16)
    x_all[ex] = x_ref[...]
    kv_all[me] = jnp.zeros(kv_all.shape[1:], BF16)
    pl.semaphore_wait(barrier, S - 1 + E - 1)

    def send_x(d):
        peer = lax.rem(ex + d, E)
        exp_copy(x_ref, x_all.at[ex], x_ss.at[peer], x_rs.at[ex], peer).start()
    loop(1, E, send_x)

    def send_kv(peer):
        want = jnp.int32(0)
        for r in range(nb):
            for j in range(TOPK):
                t = chosen_ref[peer * nb + r, j] - me * nb
                want = jnp.where((t >= 0) & (t < nb), t, want)
        kv_send[peer, 0] = k_ref[want]
        kv_send[peer, 1] = v_ref[want]
        seq_copy(pool_send, pool_all.at[me], pool_ss.at[peer], pool_rs.at[me], peer).start()
        seq_copy(kv_send.at[peer], kv_all.at[me], kv_ss.at[peer], kv_rs.at[me], peer).start()

    def send_later(i):
        peer = S - 1 - i

        @pl.when(peer > me)
        def _():
            send_kv(peer)
    loop(0, S - 1, send_later)

    def near(tile):
        q0 = tile * TILE
        width = q0 + TILE
        causal = (
            lax.broadcasted_iota(jnp.int32, (TILE, width), 0) + q0
            >= lax.broadcasted_iota(jnp.int32, (TILE, width), 1)
        )
        for h in range(heads):
            cols = slice(h * HEAD, (h + 1) * HEAD)
            s = across(
                q_ref[q0:width, cols], k_ref[0:width // GROUP, :, cols].reshape(width, HEAD)) * scale
            s = jnp.where(causal, s, NEGATIVE)
            m = jnp.max(s, axis=1, keepdims=True)
            p = jnp.exp(s - m)
            l = jnp.sum(p, axis=1, keepdims=True)
            acc[q0:width, cols] = jnp.dot(
                p.astype(BF16), v_ref[0:width // GROUP, :, cols].reshape(width, HEAD), preferred_element_type=F32)
            top[h, q0:width] = jnp.broadcast_to(m, (TILE, HEAD))
            den[h, q0:width] = jnp.broadcast_to(l, (TILE, HEAD))

    def far(b):
        r0 = pl.multiple_of(b * GROUP, GROUP)
        npool = S * nb
        width = npool + TOPK * GROUP
        col = lax.broadcasted_iota(jnp.int32, (GROUP, width), 1)
        ok = col < me * nb
        sel_k, sel_v = [], []
        for j in range(TOPK):
            c = chosen_ref[me * nb + b, j]
            low = npool + j * GROUP
            limit = jnp.where(c >= 0, low + GROUP, low)
            ok = ok | ((col >= low) & (col < limit))
            src = lax.div(jnp.maximum(c, 0), nb)
            pair = kv_all[src]
            sel_k.append(pair[0])
            sel_v.append(pair[1])
        kk = jnp.concatenate([pool_k[...]] + sel_k, axis=0)
        vv = jnp.concatenate([pool_v[...]] + sel_v, axis=0)
        for h in range(heads):
            cols = slice(h * HEAD, (h + 1) * HEAD)
            s = across(q_ref[pl.ds(r0, GROUP), cols], kk[:, cols]) * scale
            s = jnp.where(ok, s, NEGATIVE)
            m0 = top[h, pl.ds(r0, GROUP)][:, 0:1]
            l0 = den[h, pl.ds(r0, GROUP)][:, 0:1]
            m = jnp.maximum(m0, jnp.max(s, axis=1, keepdims=True))
            p = jnp.exp(s - m)
            a = jnp.exp(m0 - m)
            l = l0 * a + jnp.sum(p, axis=1, keepdims=True)
            mixed = acc[pl.ds(r0, GROUP), cols] * a + jnp.dot(
                p.astype(BF16), vv[:, cols], preferred_element_type=F32)
            mixed = mixed / l
            mean = jnp.mean(mixed * mixed, axis=1, keepdims=True)
            attn_ref[pl.ds(r0, GROUP), cols] = (
                mixed * lax.rsqrt(mean + EPSILON) * gain_ref[0:1, cols]).astype(BF16)

    tiles = L // TILE
    early = tiles - 1
    for tile in range(early):
        near(tile)

    def wait_x(d):
        src = lax.rem(ex + d, E)
        exp_copy(x_ref, x_all.at[src], x_ss.at[src], x_rs.at[src], src).wait_recv()
    loop(1, E, wait_x)
    weight_copies[0].wait()
    weight_copies[1].wait()
    x = x_all[...].reshape(rows, Dl)
    chunk = 512

    def gate_up(n):
        c0 = pl.multiple_of(n * chunk, chunk)
        g = jnp.dot(x, wg[:, pl.ds(c0, chunk)], preferred_element_type=F32)
        u = jnp.dot(x, wu[:, pl.ds(c0, chunk)], preferred_element_type=F32)
        both = jnp.concatenate([g.reshape(S, own, chunk), u.reshape(S, own, chunk)], axis=1)
        part[:, :, pl.ds(c0, chunk)] = both.astype(BF16)
    loop(0, FF // chunk, gate_up)

    def send_rs(d):
        peer = lax.rem(me + d, S)
        seq_copy(part.at[peer], rs_all.at[me], rs_ss.at[peer], rs_rs.at[me], peer).start()
    loop(1, S, send_rs)

    for tile in range(early, tiles):
        near(tile)

    def wait_rs(d, total):
        src = lax.rem(me + d, S)
        seq_copy(part.at[src], rs_all.at[src], rs_ss.at[src], rs_rs.at[src], src).wait_recv()
        return total + rs_all[src].astype(F32)
    total = lax.fori_loop(1, S, wait_rs, part[me].astype(F32))
    g, u = total[:own], total[own:]
    hidden = (g / (1.0 + jnp.exp(-g)) * u).astype(BF16)
    hid_send[...] = hidden
    hid_all[me] = hidden

    def send_hid(d):
        peer = lax.rem(me + d, S)
        seq_copy(hid_send, hid_all.at[me], hid_ss.at[peer], hid_rs.at[me], peer).start()
    loop(1, S, send_hid)

    def wait_kv(src):
        @pl.when(src < me)
        def _():
            seq_copy(pool_send, pool_all.at[src], pool_ss.at[src], pool_rs.at[src], src).wait_recv()
            seq_copy(kv_send.at[src], kv_all.at[src], kv_ss.at[src], kv_rs.at[src], src).wait_recv()
    loop(0, S - 1, wait_kv)
    pools = pool_all[...].astype(F32)
    known = lax.broadcasted_iota(jnp.int32, pools.shape, 0) < me
    pools = jnp.where(known, pools, 0.0)
    pool_k[...] = pools[:, :nb].reshape(S * nb, C).astype(BF16)
    pool_v[...] = pools[:, nb:].reshape(S * nb, C).astype(BF16)
    half = nb // 2
    loop(0, half, far)

    def wait_hid(d):
        src = lax.rem(me + d, S)
        seq_copy(hid_send, hid_all.at[src], hid_ss.at[src], hid_rs.at[src], src).wait_recv()
    loop(1, S, wait_hid)
    weight_copies[2].wait()
    hid = hid_all[...].astype(F32).reshape(rows, FF).astype(BF16)
    out = jnp.dot(hid, wd[...], preferred_element_type=F32).astype(BF16).reshape(E, T, Dl)
    ret_send[...] = out
    ret_all[ex] = ret_send[ex]

    def send_ret(d):
        peer = lax.rem(ex + d, E)
        exp_copy(ret_send.at[peer], ret_all.at[ex], ret_ss.at[peer], ret_rs.at[ex], peer).start()
    loop(1, E, send_ret)
    loop(half, nb, far)

    def wait_ret(d):
        src = lax.rem(ex + d, E)
        exp_copy(ret_send.at[src], ret_all.at[src], ret_ss.at[src], ret_rs.at[src], src).wait_recv()
    loop(1, E, wait_ret)
    ids = ids_ref[...]
    rw = rw_ref[...]
    moe = jnp.zeros((T, Dl), F32)
    for e in range(E):
        coefficient = jnp.sum(jnp.where(ids == e, rw, 0.0), axis=1, keepdims=True)
        moe = moe + coefficient * ret_all[e].astype(F32)
    moe_ref[...] = moe.astype(BF16)

    def finish_exp(d):
        peer = lax.rem(ex + d, E)
        exp_copy(x_ref, x_all.at[ex], x_ss.at[peer], x_rs.at[ex], peer).wait_send()
        exp_copy(ret_send.at[peer], ret_all.at[ex], ret_ss.at[peer], ret_rs.at[ex], peer).wait_send()
    loop(1, E, finish_exp)

    def finish_seq(d):
        peer = lax.rem(me + d, S)
        seq_copy(part.at[peer], rs_all.at[me], rs_ss.at[peer], rs_rs.at[me], peer).wait_send()
        seq_copy(hid_send, hid_all.at[me], hid_ss.at[peer], hid_rs.at[me], peer).wait_send()

        @pl.when(peer > me)
        def _():
            seq_copy(pool_send, pool_all.at[me], pool_ss.at[peer], pool_rs.at[me], peer).wait_send()
            seq_copy(kv_send.at[peer], kv_all.at[me], kv_ss.at[peer], kv_rs.at[me], peer).wait_send()
    loop(1, S, finish_seq)


def local(S, E, queries, keys, values, head_gain, chosen, moe_input, expert_ids, route_weight, w_gate, w_up, w_down):
    L, C = queries.shape
    heads = C // HEAD
    nb = L // GROUP
    T, Dl = moe_input.shape
    FF = w_gate.shape[2]
    own = E * T // S
    vmem = pl.BlockSpec(memory_space=pltpu.VMEM)
    smem = pl.BlockSpec(memory_space=pltpu.SMEM)
    hbm = pl.BlockSpec(memory_space=pl.ANY)
    dma = pltpu.SemaphoreType.DMA
    return pl.pallas_call(
        functools.partial(kernel, S, E),
        out_shape=(
            jax.ShapeDtypeStruct((L, C), BF16),
            jax.ShapeDtypeStruct((T, Dl), BF16),
        ),
        in_specs=[vmem, vmem, vmem, vmem, smem, vmem, vmem, vmem, hbm, hbm, hbm],
        out_specs=(vmem, vmem),
        scratch_shapes=[
            pltpu.VMEM((Dl, FF), BF16),
            pltpu.VMEM((Dl, FF), BF16),
            pltpu.VMEM((FF, Dl), BF16),
            pltpu.VMEM((S, 2, GROUP, C), BF16),
            pltpu.VMEM((S, 2, GROUP, C), BF16),
            pltpu.VMEM((2 * nb, C), BF16),
            pltpu.VMEM((S, 2 * nb, C), BF16),
            pltpu.VMEM((S * nb, C), BF16),
            pltpu.VMEM((S * nb, C), BF16),
            pltpu.VMEM((L, C), F32),
            pltpu.VMEM((heads, L, HEAD), F32),
            pltpu.VMEM((heads, L, HEAD), F32),
            pltpu.VMEM((E, T, Dl), BF16),
            pltpu.VMEM((S, 2 * own, FF), BF16),
            pltpu.VMEM((S, 2 * own, FF), BF16),
            pltpu.VMEM((own, FF), BF16),
            pltpu.VMEM((S, own, FF), BF16),
            pltpu.VMEM((E, T, Dl), BF16),
            pltpu.VMEM((E, T, Dl), BF16),
            dma((3,)),
            dma((S,)), dma((S,)), dma((S,)), dma((S,)),
            dma((E,)), dma((E,)),
            dma((S,)), dma((S,)), dma((S,)), dma((S,)),
            dma((E,)), dma((E,)),
        ],
        compiler_params=pltpu.CompilerParams(
            collective_id=0, has_side_effects=True, vmem_limit_bytes=56 * 1024 * 1024
        ),
    )(
        queries, keys.reshape(nb, GROUP, C), values.reshape(nb, GROUP, C), head_gain.reshape(1, C), chosen, moe_input,
        expert_ids, route_weight, w_gate[0], w_up[0], w_down[0],
    )


def solution(mesh):
    placed = (
        P("seq", "exp"),
        P("seq", "exp"),
        P("seq", "exp"),
        P("exp"),
        P(),
        P("exp", "seq"),
        P("exp", None),
        P("exp", None),
        P("exp", "seq", None),
        P("exp", "seq", None),
        P("exp", None, "seq"),
    )
    return jax.shard_map(
        functools.partial(local, mesh.shape["seq"], mesh.shape["exp"]),
        mesh=mesh,
        in_specs=placed,
        out_specs=(P("seq", "exp"), P("exp", "seq")),
        check_vma=False,
    )
```

```python
import functools

import jax
import jax.numpy as jnp
from jax import lax
from jax.experimental import pallas as pl
from jax.experimental.pallas import tpu as pltpu
from jax.sharding import PartitionSpec as P

HEAD = 128
GROUP = 64
TOPK = 3
TILE = 128
CHUNK = 512
EPSILON = 1e-06
NEGATIVE = -1e30
MESH = pl.DeviceIdType.MESH
F32 = jnp.float32
BF16 = jnp.bfloat16


def across(a, b):
    return lax.dot_general(a, b, (((1,), (1,)), ((), ())), preferred_element_type=F32)


def kernel(
    S, E,
    q_hbm, k_hbm, v_hbm, gain_ref, chosen_ref, x_ref, ids_ref, rw_ref, wg_hbm, wu_hbm, wd_hbm,
    attn_ref, moe_ref,
    q_ref, k_ref, v_ref, wg, wu, wd, k_send, k_all, v_send, v_all, pool_send, pool_all, pool_k, pool_v,
    acc, top, den, x_all, kept, pair_send, pair_all, rs_send, rs_all, hid_send, hid_all, ret_send, ret_all,
    w_sem, k_ss, k_rs, v_ss, v_rs, pool_ss, pool_rs, x_ss, x_rs, pair_ss, pair_rs, rs_ss, rs_rs,
    hid_ss, hid_rs, ret_ss, ret_rs,
):
    me = lax.axis_index("seq")
    ex = lax.axis_index("exp")
    L, C = q_hbm.shape
    heads = C // HEAD
    nb = L // GROUP
    T, Dl = x_ref.shape
    FF = wg.shape[1]
    rows = E * T
    own = rows // S
    scale = HEAD ** (-0.5)

    weight_copies = [
        pltpu.make_async_copy(src, dst, w_sem.at[i])
        for i, (src, dst) in enumerate((
            (wg_hbm, wg), (wu_hbm, wu), (wd_hbm, wd),
            (k_hbm, k_ref), (v_hbm, v_ref), (q_hbm, q_ref),
        ))
    ]
    for i in (3, 4, 5, 0, 1, 2):
        weight_copies[i].start()

    def seq_copy(src, dst, ss, rs, peer):
        return pltpu.make_async_remote_copy(
            src_ref=src, dst_ref=dst, send_sem=ss, recv_sem=rs,
            device_id={"seq": peer}, device_id_type=MESH,
        )

    def exp_copy(src, dst, ss, rs, peer):
        return pltpu.make_async_remote_copy(
            src_ref=src, dst_ref=dst, send_sem=ss, recv_sem=rs,
            device_id={"exp": peer}, device_id_type=MESH,
        )

    def loop(low, high, body):
        def step(i, c):
            body(i)
            return c
        lax.fori_loop(low, high, step, 0)

    barrier = pltpu.get_barrier_semaphore()
    loop(1, E, lambda d: pl.semaphore_signal(
        barrier, inc=1, device_id={"exp": lax.rem(ex + d, E)}, device_id_type=MESH))
    loop(1, S, lambda d: pl.semaphore_signal(
        barrier, inc=1, device_id={"seq": lax.rem(me + d, S)}, device_id_type=MESH))

    x_all[ex] = x_ref[...]
    pl.semaphore_wait(barrier, S - 1 + E - 1)

    def send_x(d):
        peer = lax.rem(ex + d, E)
        exp_copy(x_ref, x_all.at[ex], x_ss.at[peer], x_rs.at[ex], peer).start()
    loop(1, E, send_x)

    weight_copies[3].wait()
    weight_copies[4].wait()
    total_k = jnp.sum(k_ref[...].astype(F32), axis=1)
    total_v = jnp.sum(v_ref[...].astype(F32), axis=1)
    pool_send[...] = (jnp.concatenate([total_k, total_v], axis=0) * GROUP ** (-0.5)).astype(BF16)
    k_all[me] = jnp.zeros(k_all.shape[1:], BF16)
    v_all[me] = jnp.zeros(v_all.shape[1:], BF16)

    def send_kv(peer):
        want = jnp.int32(0)
        for r in range(nb):
            for j in range(TOPK):
                t = chosen_ref[j, peer * nb + r] - me * nb
                want = jnp.where((t >= 0) & (t < nb), t, want)
        k_send[peer] = k_ref[want]
        v_send[peer] = v_ref[want]
        seq_copy(pool_send, pool_all.at[me], pool_ss.at[peer], pool_rs.at[me], peer).start()
        seq_copy(k_send.at[peer], k_all.at[me], k_ss.at[peer], k_rs.at[me], peer).start()

    def send_later(i):
        peer = S - 1 - i

        @pl.when(peer > me)
        def _():
            send_kv(peer)
    loop(0, S - 1, send_later)

    def send_values(i):
        peer = S - 1 - i

        @pl.when(peer > me)
        def _():
            seq_copy(v_send.at[peer], v_all.at[me], v_ss.at[peer], v_rs.at[me], peer).start()
    loop(0, S - 1, send_values)
    weight_copies[5].wait()

    def near(tile):
        q0 = tile * TILE
        width = q0 + TILE
        causal = (
            lax.broadcasted_iota(jnp.int32, (TILE, width), 0) + q0
            >= lax.broadcasted_iota(jnp.int32, (TILE, width), 1)
        )
        for h in range(heads):
            cols = slice(h * HEAD, (h + 1) * HEAD)
            s = across(
                q_ref[q0:width, cols], k_ref[0:width // GROUP, :, cols].reshape(width, HEAD)) * scale
            s = jnp.where(causal, s, NEGATIVE)
            m = jnp.max(s, axis=1, keepdims=True)
            p = jnp.exp(s - m)
            l = jnp.sum(p, axis=1, keepdims=True)
            acc[q0:width, cols] = jnp.dot(
                p.astype(BF16), v_ref[0:width // GROUP, :, cols].reshape(width, HEAD), preferred_element_type=F32)
            top[h, q0:width] = jnp.broadcast_to(m, (TILE, HEAD))
            den[h, q0:width] = jnp.broadcast_to(l, (TILE, HEAD))

    def far(b):
        r0 = pl.multiple_of(b * GROUP, GROUP)
        npool = S * nb
        width = npool + TOPK * GROUP
        col = lax.broadcasted_iota(jnp.int32, (GROUP, width), 1)
        ok = col < me * nb
        sel_k, sel_v = [], []
        for j in range(TOPK):
            c = chosen_ref[j, me * nb + b]
            low = npool + j * GROUP
            limit = jnp.where(c >= 0, low + GROUP, low)
            ok = ok | ((col >= low) & (col < limit))
            src = lax.div(jnp.maximum(c, 0), nb)
            sel_k.append(k_all[src])
            sel_v.append(v_all[src])
        kk = jnp.concatenate([pool_k[...]] + sel_k, axis=0)
        vv = jnp.concatenate([pool_v[...]] + sel_v, axis=0)
        for h in range(heads):
            cols = slice(h * HEAD, (h + 1) * HEAD)
            s = across(q_ref[pl.ds(r0, GROUP), cols], kk[:, cols]) * scale
            s = jnp.where(ok, s, NEGATIVE)
            m0 = top[h, pl.ds(r0, GROUP)][:, 0:1]
            l0 = den[h, pl.ds(r0, GROUP)][:, 0:1]
            m = jnp.maximum(m0, jnp.max(s, axis=1, keepdims=True))
            p = jnp.exp(s - m)
            a = jnp.exp(m0 - m)
            l = l0 * a + jnp.sum(p, axis=1, keepdims=True)
            mixed = acc[pl.ds(r0, GROUP), cols] * a + jnp.dot(
                p.astype(BF16), vv[:, cols], preferred_element_type=F32)
            mixed = mixed / l
            mean = jnp.mean(mixed * mixed, axis=1, keepdims=True)
            attn_ref[pl.ds(r0, GROUP), cols] = (
                mixed * lax.rsqrt(mean + EPSILON) * gain_ref[0:1, cols]).astype(BF16)

    tiles = L // TILE
    early = tiles - 1
    for tile in range(early):
        near(tile)

    def wait_x(d):
        src = lax.rem(ex + d, E)
        exp_copy(x_ref, x_all.at[src], x_ss.at[src], x_rs.at[src], src).wait_recv()
    loop(1, E, wait_x)
    weight_copies[0].wait()
    weight_copies[1].wait()
    x = x_all[...].reshape(rows, Dl)
    chunk = CHUNK

    chunks = FF // chunk
    pairs = S // 2
    side = lax.rem(me, 2)
    spot = lax.div(me, 2)
    partner = me + 1 - 2 * side

    def pair_copy(n):
        return seq_copy(pair_send.at[n], pair_all.at[n], pair_ss.at[n], pair_rs.at[n], partner)

    def gate_up(n):
        c0 = pl.multiple_of(n * chunk, chunk)
        g = jnp.dot(x, wg[:, pl.ds(c0, chunk)], preferred_element_type=F32)
        u = jnp.dot(x, wu[:, pl.ds(c0, chunk)], preferred_element_type=F32)
        both = jnp.concatenate([g.reshape(S, own, chunk), u.reshape(S, own, chunk)], axis=1)
        both = both.reshape(pairs, 2, 2 * own, chunk)
        kept[n] = jnp.where(side == 0, both[:, 0], both[:, 1])
        pair_send[n] = jnp.where(side == 0, both[:, 1], both[:, 0])
        pair_copy(n).start()
    loop(0, chunks, gate_up)

    def rs_copy(n, d, sender, receiver):
        return seq_copy(
            rs_send.at[n, receiver], rs_all.at[n, sender],
            rs_ss.at[n, receiver], rs_rs.at[n, sender], 2 * receiver + side)

    def send_rs(n):
        pair_copy(n).wait_recv()
        both = kept[n] + pair_all[n]
        kept[n] = both
        rs_send[n] = both.astype(BF16)

        def each(d):
            rs_copy(n, d, spot, lax.rem(spot + d, pairs)).start()
        loop(1, pairs, each)
    loop(0, chunks, send_rs)

    for tile in range(early, tiles):
        near(tile)

    def wait_rs(n):
        total = kept[n, spot]

        def each(d, total):
            src = lax.rem(spot + d, pairs)
            seq_copy(
                rs_send.at[n, src], rs_all.at[n, src], rs_ss.at[n, src], rs_rs.at[n, src],
                2 * src + side).wait_recv()
            return total + rs_all[n, src].astype(F32)
        total = lax.fori_loop(1, pairs, each, total)
        g, u = total[:own], total[own:]
        hidden = (g / (1.0 + jnp.exp(-g)) * u).astype(BF16)
        c0 = pl.multiple_of(n * chunk, chunk)
        hid_send[:, pl.ds(c0, chunk)] = hidden
    loop(0, chunks, wait_rs)
    hid_all[me] = hid_send[...]

    def send_hid(d):
        peer = lax.rem(me + d, S)
        seq_copy(hid_send, hid_all.at[me], hid_ss.at[peer], hid_rs.at[me], peer).start()
    loop(1, S, send_hid)

    def wait_kv(src):
        @pl.when(src < me)
        def _():
            seq_copy(pool_send, pool_all.at[src], pool_ss.at[src], pool_rs.at[src], src).wait_recv()
            seq_copy(k_send.at[src], k_all.at[src], k_ss.at[src], k_rs.at[src], src).wait_recv()
            seq_copy(v_send.at[src], v_all.at[src], v_ss.at[src], v_rs.at[src], src).wait_recv()
    loop(0, S - 1, wait_kv)
    pools = pool_all[...].astype(F32)
    known = lax.broadcasted_iota(jnp.int32, pools.shape, 0) < me
    pools = jnp.where(known, pools, 0.0)
    pool_k[...] = pools[:, :nb].reshape(S * nb, C).astype(BF16)
    pool_v[...] = pools[:, nb:].reshape(S * nb, C).astype(BF16)
    half = nb // 2
    loop(0, half, far)

    def wait_hid(d):
        src = lax.rem(me + d, S)
        seq_copy(hid_send, hid_all.at[src], hid_ss.at[src], hid_rs.at[src], src).wait_recv()
    loop(1, S, wait_hid)
    weight_copies[2].wait()
    hid = hid_all[...].astype(F32).reshape(rows, FF).astype(BF16)
    out = jnp.dot(hid, wd[...], preferred_element_type=F32).astype(BF16).reshape(E, T, Dl)
    ret_send[...] = out
    ret_all[ex] = ret_send[ex]

    def send_ret(d):
        peer = lax.rem(ex + d, E)
        exp_copy(ret_send.at[peer], ret_all.at[ex], ret_ss.at[peer], ret_rs.at[ex], peer).start()
    loop(1, E, send_ret)
    loop(half, nb, far)

    ids = ids_ref[...]
    rw = rw_ref[...]
    diagonal = (
        lax.broadcasted_iota(jnp.int32, (T, T), 0) == lax.broadcasted_iota(jnp.int32, (T, T), 1)
    )
    coefficients = []
    for e in range(E):
        row = jnp.sum(jnp.where(ids == e, rw, 0.0), axis=0, keepdims=True)
        square = jnp.where(diagonal, jnp.broadcast_to(row, (T, T)), 0.0)
        coefficients.append(jnp.sum(square, axis=1, keepdims=True))

    def wait_ret(d):
        src = lax.rem(ex + d, E)
        exp_copy(ret_send.at[src], ret_all.at[src], ret_ss.at[src], ret_rs.at[src], src).wait_recv()
    loop(1, E, wait_ret)
    moe = jnp.zeros((T, Dl), F32)
    for e in range(E):
        moe = moe + coefficients[e] * ret_all[e].astype(F32)
    moe_ref[...] = moe.astype(BF16)

    def finish_exp(d):
        peer = lax.rem(ex + d, E)
        exp_copy(x_ref, x_all.at[ex], x_ss.at[peer], x_rs.at[ex], peer).wait_send()
        exp_copy(ret_send.at[peer], ret_all.at[ex], ret_ss.at[peer], ret_rs.at[ex], peer).wait_send()
    loop(1, E, finish_exp)

    def finish_seq(d):
        peer = lax.rem(me + d, S)
        seq_copy(hid_send, hid_all.at[me], hid_ss.at[peer], hid_rs.at[me], peer).wait_send()

        @pl.when(peer > me)
        def _():
            seq_copy(pool_send, pool_all.at[me], pool_ss.at[peer], pool_rs.at[me], peer).wait_send()
            seq_copy(k_send.at[peer], k_all.at[me], k_ss.at[peer], k_rs.at[me], peer).wait_send()
            seq_copy(v_send.at[peer], v_all.at[me], v_ss.at[peer], v_rs.at[me], peer).wait_send()
    loop(1, S, finish_seq)

    def finish_rs(n):
        pair_copy(n).wait_send()
        loop(1, pairs, lambda d: rs_copy(n, d, spot, lax.rem(spot + d, pairs)).wait_send())
    loop(0, chunks, finish_rs)


def local(S, E, queries, keys, values, head_gain, chosen, moe_input, expert_ids, route_weight, w_gate, w_up, w_down):
    L, C = queries.shape
    heads = C // HEAD
    nb = L // GROUP
    T, Dl = moe_input.shape
    FF = w_gate.shape[2]
    own = E * T // S
    chunks = FF // CHUNK
    vmem = pl.BlockSpec(memory_space=pltpu.VMEM)
    smem = pl.BlockSpec(memory_space=pltpu.SMEM)
    hbm = pl.BlockSpec(memory_space=pl.ANY)
    dma = pltpu.SemaphoreType.DMA
    return pl.pallas_call(
        functools.partial(kernel, S, E),
        out_shape=(
            jax.ShapeDtypeStruct((L, C), BF16),
            jax.ShapeDtypeStruct((T, Dl), BF16),
        ),
        in_specs=[hbm, hbm, hbm, vmem, smem, vmem, vmem, vmem, hbm, hbm, hbm],
        out_specs=(vmem, vmem),
        scratch_shapes=[
            pltpu.VMEM((L, C), BF16),
            pltpu.VMEM((nb, GROUP, C), BF16),
            pltpu.VMEM((nb, GROUP, C), BF16),
            pltpu.VMEM((Dl, FF), BF16),
            pltpu.VMEM((Dl, FF), BF16),
            pltpu.VMEM((FF, Dl), BF16),
            pltpu.VMEM((S, GROUP, C), BF16),
            pltpu.VMEM((S, GROUP, C), BF16),
            pltpu.VMEM((S, GROUP, C), BF16),
            pltpu.VMEM((S, GROUP, C), BF16),
            pltpu.VMEM((2 * nb, C), BF16),
            pltpu.VMEM((S, 2 * nb, C), BF16),
            pltpu.VMEM((S * nb, C), BF16),
            pltpu.VMEM((S * nb, C), BF16),
            pltpu.VMEM((L, C), F32),
            pltpu.VMEM((heads, L, HEAD), F32),
            pltpu.VMEM((heads, L, HEAD), F32),
            pltpu.VMEM((E, T, Dl), BF16),
            pltpu.VMEM((chunks, S // 2, 2 * own, CHUNK), F32),
            pltpu.VMEM((chunks, S // 2, 2 * own, CHUNK), F32),
            pltpu.VMEM((chunks, S // 2, 2 * own, CHUNK), F32),
            pltpu.VMEM((chunks, S // 2, 2 * own, CHUNK), BF16),
            pltpu.VMEM((chunks, S // 2, 2 * own, CHUNK), BF16),
            pltpu.VMEM((own, FF), BF16),
            pltpu.VMEM((S, own, FF), BF16),
            pltpu.VMEM((E, T, Dl), BF16),
            pltpu.VMEM((E, T, Dl), BF16),
            dma((6,)),
            dma((S,)), dma((S,)), dma((S,)), dma((S,)), dma((S,)), dma((S,)),
            dma((E,)), dma((E,)),
            dma((chunks,)), dma((chunks,)), dma((chunks, S // 2)), dma((chunks, S // 2)),
            dma((S,)), dma((S,)),
            dma((E,)), dma((E,)),
        ],
        compiler_params=pltpu.CompilerParams(
            collective_id=0, has_side_effects=True, vmem_limit_bytes=56 * 1024 * 1024
        ),
    )(
        queries, keys.reshape(nb, GROUP, C), values.reshape(nb, GROUP, C), head_gain.reshape(1, C), chosen.T, moe_input,
        expert_ids.T, route_weight.T, w_gate[0], w_up[0], w_down[0],
    )


def solution(mesh):
    placed = (
        P("seq", "exp"),
        P("seq", "exp"),
        P("seq", "exp"),
        P("exp"),
        P(),
        P("exp", "seq"),
        P("exp", None),
        P("exp", None),
        P("exp", "seq", None),
        P("exp", "seq", None),
        P("exp", None, "seq"),
    )
    return jax.shard_map(
        functools.partial(local, mesh.shape["seq"], mesh.shape["exp"]),
        mesh=mesh,
        in_specs=placed,
        out_specs=(P("seq", "exp"), P("exp", "seq")),
        check_vma=False,
    )
```

```python
import functools

import jax
import jax.numpy as jnp
from jax import lax
from jax.experimental import pallas as pl
from jax.experimental.pallas import tpu as pltpu
from jax.sharding import PartitionSpec as P

HEAD = 128
GROUP = 64
FAR = 2
TOPK = 3
TILE = 128
CHUNK = 512
EPSILON = 1e-06
NEGATIVE = -1e30
MESH = pl.DeviceIdType.MESH
F32 = jnp.float32
BF16 = jnp.bfloat16


def across(a, b):
    return lax.dot_general(a, b, (((1,), (1,)), ((), ())), preferred_element_type=F32)


def kernel(
    S, E,
    q_hbm, k_hbm, v_hbm, gain_ref, chosen_ref, x_ref, ids_ref, rw_ref, wg_hbm, wu_hbm, wd_hbm,
    attn_ref, moe_ref,
    q_ref, k_ref, v_ref, wg, wu, wd, k_send, k_all, v_send, v_all, pool_send, pool_all, pool_k, pool_v,
    acc, top, den, x_all, kept, pair_send, pair_all, rs_send, rs_all, hid_send, hid_all, ret_send, ret_all,
    w_sem, k_ss, k_rs, v_ss, v_rs, pool_ss, pool_rs, x_ss, x_rs, pair_ss, pair_rs, rs_ss, rs_rs,
    hid_ss, hid_rs, ret_ss, ret_rs,
):
    me = lax.axis_index("seq")
    ex = lax.axis_index("exp")
    L, C = q_hbm.shape
    heads = C // HEAD
    nb = L // GROUP
    T, Dl = x_ref.shape
    FF = wg.shape[1]
    rows = E * T
    own = rows // S
    scale = HEAD ** (-0.5)

    weight_copies = [
        pltpu.make_async_copy(src, dst, w_sem.at[i])
        for i, (src, dst) in enumerate((
            (wg_hbm, wg), (wu_hbm, wu), (wd_hbm, wd),
            (k_hbm, k_ref), (v_hbm, v_ref), (q_hbm, q_ref),
        ))
    ]
    for i in (3, 4, 5, 0, 1, 2):
        weight_copies[i].start()

    def seq_copy(src, dst, ss, rs, peer):
        return pltpu.make_async_remote_copy(
            src_ref=src, dst_ref=dst, send_sem=ss, recv_sem=rs,
            device_id={"seq": peer}, device_id_type=MESH,
        )

    def exp_copy(src, dst, ss, rs, peer):
        return pltpu.make_async_remote_copy(
            src_ref=src, dst_ref=dst, send_sem=ss, recv_sem=rs,
            device_id={"exp": peer}, device_id_type=MESH,
        )

    def loop(low, high, body):
        def step(i, c):
            body(i)
            return c
        lax.fori_loop(low, high, step, 0)

    barrier = pltpu.get_barrier_semaphore()
    loop(1, E, lambda d: pl.semaphore_signal(
        barrier, inc=1, device_id={"exp": lax.rem(ex + d, E)}, device_id_type=MESH))
    loop(1, S, lambda d: pl.semaphore_signal(
        barrier, inc=1, device_id={"seq": lax.rem(me + d, S)}, device_id_type=MESH))

    x_all[ex] = x_ref[...]
    pl.semaphore_wait(barrier, S - 1 + E - 1)

    def send_x(d):
        peer = lax.rem(ex + d, E)
        exp_copy(x_ref, x_all.at[ex], x_ss.at[peer], x_rs.at[ex], peer).start()
    loop(1, E, send_x)

    weight_copies[3].wait()
    weight_copies[4].wait()
    total_k = jnp.sum(k_ref[...].astype(F32), axis=1)
    total_v = jnp.sum(v_ref[...].astype(F32), axis=1)
    pool_send[...] = (jnp.concatenate([total_k, total_v], axis=0) * GROUP ** (-0.5)).astype(BF16)
    k_all[me] = jnp.zeros(k_all.shape[1:], BF16)
    v_all[me] = jnp.zeros(v_all.shape[1:], BF16)

    def send_kv(peer):
        want = jnp.int32(0)
        for r in range(nb):
            for j in range(TOPK):
                t = chosen_ref[j, peer * nb + r] - me * nb
                want = jnp.where((t >= 0) & (t < nb), t, want)
        k_send[peer] = k_ref[want]
        v_send[peer] = v_ref[want]
        seq_copy(pool_send, pool_all.at[me], pool_ss.at[peer], pool_rs.at[me], peer).start()
        seq_copy(k_send.at[peer], k_all.at[me], k_ss.at[peer], k_rs.at[me], peer).start()

    def send_later(i):
        peer = S - 1 - i

        @pl.when(peer > me)
        def _():
            send_kv(peer)
    loop(0, S - 1, send_later)

    def send_values(i):
        peer = S - 1 - i

        @pl.when(peer > me)
        def _():
            seq_copy(v_send.at[peer], v_all.at[me], v_ss.at[peer], v_rs.at[me], peer).start()
    weight_copies[5].wait()

    def near(tile):
        q0 = tile * TILE
        width = q0 + TILE
        causal = (
            lax.broadcasted_iota(jnp.int32, (TILE, width), 0) + q0
            >= lax.broadcasted_iota(jnp.int32, (TILE, width), 1)
        )
        for h in range(heads):
            cols = slice(h * HEAD, (h + 1) * HEAD)
            s = across(
                q_ref[q0:width, cols], k_ref[0:width // GROUP, :, cols].reshape(width, HEAD)) * scale
            s = jnp.where(causal, s, NEGATIVE)
            m = jnp.max(s, axis=1, keepdims=True)
            p = jnp.exp(s - m)
            l = jnp.sum(p, axis=1, keepdims=True)
            acc[q0:width, cols] = jnp.dot(
                p.astype(BF16), v_ref[0:width // GROUP, :, cols].reshape(width, HEAD), preferred_element_type=F32)
            top[h, q0:width] = jnp.broadcast_to(m, (TILE, HEAD))
            den[h, q0:width] = jnp.broadcast_to(l, (TILE, HEAD))

    def far(step):
        npool = S * nb
        width = npool + TOPK * GROUP
        col = lax.broadcasted_iota(jnp.int32, (GROUP, width), 1)
        work = []
        for i in range(FAR):
            b = step * FAR + i
            r0 = pl.multiple_of(b * GROUP, GROUP)
            ok = col < me * nb
            srcs = []
            for j in range(TOPK):
                c = chosen_ref[j, me * nb + b]
                low = npool + j * GROUP
                limit = jnp.where(c >= 0, low + GROUP, low)
                ok = ok | ((col >= low) & (col < limit))
                srcs.append(lax.div(jnp.maximum(c, 0), nb))
            kk = jnp.concatenate([pool_k[...]] + [k_all[src] for src in srcs], axis=0)
            vv = jnp.concatenate([pool_v[...]] + [v_all[src] for src in srcs], axis=0)
            for h in range(heads):
                cols = slice(h * HEAD, (h + 1) * HEAD)
                s = across(q_ref[pl.ds(r0, GROUP), cols], kk[:, cols]) * scale
                work.append((h, r0, cols, jnp.where(ok, s, NEGATIVE), vv[:, cols]))
        tops = []
        for h, r0, cols, s, vv in work:
            m0 = top[h, pl.ds(r0, GROUP)]
            m = jnp.maximum(m0, jnp.max(s, axis=1, keepdims=True))
            tops.append((m, jnp.exp(m0 - m)))
        probs = []
        for (h, r0, cols, s, vv), (m, a) in zip(work, tops):
            wide = jnp.concatenate([m] * (-(-width // HEAD)), axis=1)[:, :width]
            p = jnp.exp(s - wide)
            l = den[h, pl.ds(r0, GROUP)] * a + jnp.sum(p, axis=1, keepdims=True)
            probs.append((p.astype(BF16), l))
        outs = []
        for (h, r0, cols, s, vv), (m, a), (p, l) in zip(work, tops, probs):
            mixed = acc[pl.ds(r0, GROUP), cols] * a + jnp.dot(p, vv, preferred_element_type=F32)
            outs.append(mixed / l)
        for (h, r0, cols, s, vv), mixed in zip(work, outs):
            mean = jnp.mean(mixed * mixed, axis=1, keepdims=True)
            attn_ref[pl.ds(r0, GROUP), cols] = (
                mixed * lax.rsqrt(mean + EPSILON) * gain_ref[0:1, cols]).astype(BF16)

    tiles = L // TILE
    early = tiles - 1
    for tile in range(early):
        near(tile)

    def wait_x(d):
        src = lax.rem(ex + d, E)
        exp_copy(x_ref, x_all.at[src], x_ss.at[src], x_rs.at[src], src).wait_recv()
    loop(1, E, wait_x)
    weight_copies[0].wait()
    weight_copies[1].wait()
    x = x_all[...].reshape(rows, Dl)
    chunk = CHUNK

    chunks = FF // chunk
    pairs = S // 2
    side = lax.rem(me, 2)
    spot = lax.div(me, 2)
    partner = me + 1 - 2 * side

    def pair_copy(n):
        return seq_copy(pair_send.at[n], pair_all.at[n], pair_ss.at[n], pair_rs.at[n], partner)

    def gate_up(n):
        c0 = pl.multiple_of(n * chunk, chunk)
        g = jnp.dot(x, wg[:, pl.ds(c0, chunk)], preferred_element_type=F32)
        u = jnp.dot(x, wu[:, pl.ds(c0, chunk)], preferred_element_type=F32)
        both = jnp.concatenate([g.reshape(S, own, chunk), u.reshape(S, own, chunk)], axis=1)
        both = both.reshape(pairs, 2, 2 * own, chunk)
        kept[n] = jnp.where(side == 0, both[:, 0], both[:, 1])
        pair_send[n] = jnp.where(side == 0, both[:, 1], both[:, 0])
        pair_copy(n).start()
    loop(0, chunks, gate_up)

    def rs_copy(n, d, sender, receiver):
        return seq_copy(
            rs_send.at[n, receiver], rs_all.at[n, sender],
            rs_ss.at[n, receiver], rs_rs.at[n, sender], 2 * receiver + side)

    def send_rs(n):
        pair_copy(n).wait_recv()
        both = kept[n] + pair_all[n]
        kept[n] = both
        rs_send[n] = both.astype(BF16)

        def each(d):
            rs_copy(n, d, spot, lax.rem(spot + d, pairs)).start()
        loop(1, pairs, each)
    loop(0, chunks, send_rs)

    for tile in range(early, tiles):
        near(tile)

    def wait_rs(n):
        total = kept[n, spot]

        def each(d, total):
            src = lax.rem(spot + d, pairs)
            seq_copy(
                rs_send.at[n, src], rs_all.at[n, src], rs_ss.at[n, src], rs_rs.at[n, src],
                2 * src + side).wait_recv()
            return total + rs_all[n, src].astype(F32)
        total = lax.fori_loop(1, pairs, each, total)
        g, u = total[:own], total[own:]
        hidden = (g / (1.0 + jnp.exp(-g)) * u).astype(BF16)
        c0 = pl.multiple_of(n * chunk, chunk)
        hid_send[:, pl.ds(c0, chunk)] = hidden
    loop(0, chunks, wait_rs)
    hid_all[me] = hid_send[...]

    def send_hid(d):
        peer = lax.rem(me + d, S)
        seq_copy(hid_send, hid_all.at[me], hid_ss.at[peer], hid_rs.at[me], peer).start()
    loop(1, S, send_hid)
    loop(0, S - 1, send_values)

    steps = nb // FAR

    def wait_hid(d):
        src = lax.rem(me + d, S)
        seq_copy(hid_send, hid_all.at[src], hid_ss.at[src], hid_rs.at[src], src).wait_recv()
    loop(1, S, wait_hid)
    weight_copies[2].wait()
    hid = hid_all[...].astype(F32).reshape(rows, FF).astype(BF16)
    out = jnp.dot(hid, wd[...], preferred_element_type=F32).astype(BF16).reshape(E, T, Dl)
    ret_send[...] = out
    ret_all[ex] = ret_send[ex]

    def send_ret(d):
        peer = lax.rem(ex + d, E)
        exp_copy(ret_send.at[peer], ret_all.at[ex], ret_ss.at[peer], ret_rs.at[ex], peer).start()
    loop(1, E, send_ret)
    def wait_kv(src):
        @pl.when(src < me)
        def _():
            seq_copy(pool_send, pool_all.at[src], pool_ss.at[src], pool_rs.at[src], src).wait_recv()
            seq_copy(k_send.at[src], k_all.at[src], k_ss.at[src], k_rs.at[src], src).wait_recv()
            seq_copy(v_send.at[src], v_all.at[src], v_ss.at[src], v_rs.at[src], src).wait_recv()
    loop(0, S - 1, wait_kv)
    pools = pool_all[...].astype(F32)
    known = lax.broadcasted_iota(jnp.int32, pools.shape, 0) < me
    pools = jnp.where(known, pools, 0.0)
    pool_k[...] = pools[:, :nb].reshape(S * nb, C).astype(BF16)
    pool_v[...] = pools[:, nb:].reshape(S * nb, C).astype(BF16)
    loop(0, steps, far)


    ids = ids_ref[...]
    rw = rw_ref[...]
    diagonal = (
        lax.broadcasted_iota(jnp.int32, (T, T), 0) == lax.broadcasted_iota(jnp.int32, (T, T), 1)
    )
    coefficients = []
    for e in range(E):
        row = jnp.sum(jnp.where(ids == e, rw, 0.0), axis=0, keepdims=True)
        square = jnp.where(diagonal, jnp.broadcast_to(row, (T, T)), 0.0)
        coefficients.append(jnp.sum(square, axis=1, keepdims=True))

    def wait_ret(d):
        src = lax.rem(ex + d, E)
        exp_copy(ret_send.at[src], ret_all.at[src], ret_ss.at[src], ret_rs.at[src], src).wait_recv()
    loop(1, E, wait_ret)
    moe = jnp.zeros((T, Dl), F32)
    for e in range(E):
        moe = moe + coefficients[e] * ret_all[e].astype(F32)
    moe_ref[...] = moe.astype(BF16)

    def finish_exp(d):
        peer = lax.rem(ex + d, E)
        exp_copy(x_ref, x_all.at[ex], x_ss.at[peer], x_rs.at[ex], peer).wait_send()
        exp_copy(ret_send.at[peer], ret_all.at[ex], ret_ss.at[peer], ret_rs.at[ex], peer).wait_send()
    loop(1, E, finish_exp)

    def finish_seq(d):
        peer = lax.rem(me + d, S)
        seq_copy(hid_send, hid_all.at[me], hid_ss.at[peer], hid_rs.at[me], peer).wait_send()

        @pl.when(peer > me)
        def _():
            seq_copy(pool_send, pool_all.at[me], pool_ss.at[peer], pool_rs.at[me], peer).wait_send()
            seq_copy(k_send.at[peer], k_all.at[me], k_ss.at[peer], k_rs.at[me], peer).wait_send()
            seq_copy(v_send.at[peer], v_all.at[me], v_ss.at[peer], v_rs.at[me], peer).wait_send()
    loop(1, S, finish_seq)

    def finish_rs(n):
        pair_copy(n).wait_send()
        loop(1, pairs, lambda d: rs_copy(n, d, spot, lax.rem(spot + d, pairs)).wait_send())
    loop(0, chunks, finish_rs)


def local(S, E, queries, keys, values, head_gain, chosen, moe_input, expert_ids, route_weight, w_gate, w_up, w_down):
    L, C = queries.shape
    heads = C // HEAD
    nb = L // GROUP
    T, Dl = moe_input.shape
    FF = w_gate.shape[2]
    own = E * T // S
    chunks = FF // CHUNK
    vmem = pl.BlockSpec(memory_space=pltpu.VMEM)
    smem = pl.BlockSpec(memory_space=pltpu.SMEM)
    hbm = pl.BlockSpec(memory_space=pl.ANY)
    dma = pltpu.SemaphoreType.DMA
    return pl.pallas_call(
        functools.partial(kernel, S, E),
        out_shape=(
            jax.ShapeDtypeStruct((L, C), BF16),
            jax.ShapeDtypeStruct((T, Dl), BF16),
        ),
        in_specs=[hbm, hbm, hbm, vmem, smem, vmem, vmem, vmem, hbm, hbm, hbm],
        out_specs=(vmem, vmem),
        scratch_shapes=[
            pltpu.VMEM((L, C), BF16),
            pltpu.VMEM((nb, GROUP, C), BF16),
            pltpu.VMEM((nb, GROUP, C), BF16),
            pltpu.VMEM((Dl, FF), BF16),
            pltpu.VMEM((Dl, FF), BF16),
            pltpu.VMEM((FF, Dl), BF16),
            pltpu.VMEM((S, GROUP, C), BF16),
            pltpu.VMEM((S, GROUP, C), BF16),
            pltpu.VMEM((S, GROUP, C), BF16),
            pltpu.VMEM((S, GROUP, C), BF16),
            pltpu.VMEM((2 * nb, C), BF16),
            pltpu.VMEM((S, 2 * nb, C), BF16),
            pltpu.VMEM((S * nb, C), BF16),
            pltpu.VMEM((S * nb, C), BF16),
            pltpu.VMEM((L, C), F32),
            pltpu.VMEM((heads, L, HEAD), F32),
            pltpu.VMEM((heads, L, HEAD), F32),
            pltpu.VMEM((E, T, Dl), BF16),
            pltpu.VMEM((chunks, S // 2, 2 * own, CHUNK), F32),
            pltpu.VMEM((chunks, S // 2, 2 * own, CHUNK), F32),
            pltpu.VMEM((chunks, S // 2, 2 * own, CHUNK), F32),
            pltpu.VMEM((chunks, S // 2, 2 * own, CHUNK), BF16),
            pltpu.VMEM((chunks, S // 2, 2 * own, CHUNK), BF16),
            pltpu.VMEM((own, FF), BF16),
            pltpu.VMEM((S, own, FF), BF16),
            pltpu.VMEM((E, T, Dl), BF16),
            pltpu.VMEM((E, T, Dl), BF16),
            dma((6,)),
            dma((S,)), dma((S,)), dma((S,)), dma((S,)), dma((S,)), dma((S,)),
            dma((E,)), dma((E,)),
            dma((chunks,)), dma((chunks,)), dma((chunks, S // 2)), dma((chunks, S // 2)),
            dma((S,)), dma((S,)),
            dma((E,)), dma((E,)),
        ],
        compiler_params=pltpu.CompilerParams(
            collective_id=0, has_side_effects=True, vmem_limit_bytes=56 * 1024 * 1024
        ),
    )(
        queries, keys.reshape(nb, GROUP, C), values.reshape(nb, GROUP, C), head_gain.reshape(1, C), chosen.T, moe_input,
        expert_ids.T, route_weight.T, w_gate[0], w_up[0], w_down[0],
    )


def solution(mesh):
    placed = (
        P("seq", "exp"),
        P("seq", "exp"),
        P("seq", "exp"),
        P("exp"),
        P(),
        P("exp", "seq"),
        P("exp", None),
        P("exp", None),
        P("exp", "seq", None),
        P("exp", "seq", None),
        P("exp", None, "seq"),
    )
    return jax.shard_map(
        functools.partial(local, mesh.shape["seq"], mesh.shape["exp"]),
        mesh=mesh,
        in_specs=placed,
        out_specs=(P("seq", "exp"), P("exp", "seq")),
        check_vma=False,
    )
```
